32 devices in a mesh: fac: 8 (over y, x, core), freq: 4 (over z).
Axes of the slice: x: 2, y: 2, z: 4, core: 2. Of those that a mesh axis runs over, the one named last changes fastest.
Arguments:
- right_side: float32 [16, 36864, 128], P('freq', 'fac'), may hold values from -6 to 6
- factors: bfloat16 [36864, 1024], P('fac'), may hold values from -0.03125 to 0.03125
- pair_weight: float32 [16, 36864], P('freq', 'fac'), may hold values from -2 to 2
- second_order: float32 [16, 36864], P('freq', 'fac'), may hold values from -1 to 1
- forward: float32 [16, 16], replicated, may hold values from -3 to 3
- backward: float32 [16, 16], replicated, may hold values from -3 to 3
Outputs:
- amplitude: float32 [16, 36864, 128], P('freq', 'fac')
- sources: float32 [16, 36864, 128], P('freq', 'fac')
The draws below stay inside these ranges and needn't reach their ends.
All inputs are finite; a program needn't handle non-finite values.
Results may differ from the reference program's by a relative error of at most 0.0015.
Values may be sent and summed in bfloat16 or wider, within the bound.
A program may use at most 128 MiB of HBM per device.

```python
import jax
import jax.numpy as jnp
from jax import lax

NAUX = 1024
NFREQ = 16
COLS = 128
OUTER = 2
INNER = 2
PAIRS = 36864


def steps_of(key, dims, shards, low, largest):
    loudness, own = 1.0, jax.random.fold_in(key, 6)
    for dim, parts in shards:
        heights = jnp.exp(jax.random.uniform(jax.random.fold_in(own, dim), (parts,), jnp.float32, low / len(shards), largest / len(shards)))
        loudness = loudness * jnp.repeat(heights, dims[dim] // parts).reshape([-1 if axis == dim else 1 for axis in range(len(dims))])
    return loudness


def scatter_about(rng, extent, width, limit, split=(), kind=jnp.bfloat16):
    values = width * jax.random.normal(rng, extent, jnp.float32)
    if split:
        values = values * steps_of(rng, extent, split, -0.22, 0.18)
    return jnp.clip(values, -limit, limit).astype(kind)


def setup_inputs(seed: int = 0) -> dict:
    seeds = jax.random.split(jax.random.key(seed), 7)
    return {
        "right_side": scatter_about(seeds[0], (NFREQ, PAIRS, COLS), 1.0, 6.0, ((0, 4), (1, 8)), jnp.float32),
        "factors": scatter_about(seeds[1], (PAIRS, NAUX), PAIRS ** -0.5, 0.03125, ((0, 8),)),
        "pair_weight": jnp.clip(jax.random.uniform(seeds[2], (NFREQ, PAIRS), jnp.float32, -2.0, 2.0) * steps_of(seeds[2], (NFREQ, PAIRS), ((0, 4), (1, 8)), -0.4, 0.0), -2.0, 2.0),
        "second_order": jnp.clip(jax.random.uniform(seeds[3], (NFREQ, PAIRS), jnp.float32, -1.0, 1.0) * steps_of(seeds[3], (NFREQ, PAIRS), ((0, 4), (1, 8)), -0.4, 0.0), -1.0, 1.0),
        "forward": scatter_about(seeds[4], (NFREQ, NFREQ), (NFREQ // 4) ** -0.5, 3.0, (), jnp.float32),
        "backward": scatter_about(seeds[5], (NFREQ, NFREQ), (NFREQ // 4) ** -0.5, 3.0, (), jnp.float32),
    }


def reference(right_side, factors, pair_weight, second_order, forward, backward):
    sources = right_side
    amplitude = sources
    for outer in range(OUTER):
        amplitude = sources
        for inner in range(INNER):
            fresh = []
            for freq in range(NFREQ):
                rounded = amplitude[freq].astype(jnp.bfloat16)
                projection = jnp.dot(factors.T, rounded, preferred_element_type=jnp.float32)
                projected = projection.astype(jnp.bfloat16)
                spread = jnp.dot(factors, projected, preferred_element_type=jnp.float32)
                fresh.append(sources[freq] + pair_weight[freq][:, None] * spread)
            amplitude = jnp.stack(fresh)
        timed = jnp.einsum("tw,wpc->tpc", forward, amplitude, precision=lax.Precision.HIGHEST)
        product = second_order[:, :, None] * timed
        returned = jnp.einsum("wt,tpc->wpc", backward, product, precision=lax.Precision.HIGHEST)
        sources = right_side + returned
    return amplitude, sources
```

```python
import functools

import jax
import jax.numpy as jnp
from jax import lax
from jax.experimental import pallas as pl
from jax.experimental.pallas import tpu as pltpu
from jax.sharding import PartitionSpec as P

OUTER = 2
INNER = 2
ROWS = 8
EXACT = lax.Precision.HIGHEST


def tile_of(pairs):
    for tile in (384, 288, 256, 192, 144, 128, 96, 72, 64, 48, 32, 16):
        if pairs % tile == 0:
            return tile
    return pairs


def mix(table, base, outs, terms):
    n = len(terms)
    result = []
    for w in range(outs):
        total = None
        for v in range(n):
            col = base + w * n + v
            term = table[:, col : col + 1] * terms[v]
            total = term if total is None else total + term
        result.append(total)
    return result


def early_kernel(nf, m_ref, x_ref, v_ref):
    tile = m_ref.shape[0]

    @pl.loop(0, tile // ROWS)
    def _(i):
        rows = pl.ds(pl.multiple_of(i * ROWS, ROWS), ROWS)
        table = m_ref[rows, :]
        got = mix(table, 0, nf, [x_ref[v, rows, :] for v in range(nf)])
        for w in range(nf):
            v_ref[w, rows, :] = got[w]


def spread_all(l_ref, p_refs, held):
    block = p_refs[0].shape[1]
    for i, p_ref in enumerate(p_refs):
        held[:, i * block : (i + 1) * block] = jnp.dot(
            l_ref[...], p_ref[...], preferred_element_type=jnp.float32
        )


def whole_kernel(nf, blocks, l_ref, m_ref, wt_ref, b_ref, *rest):
    p_refs, u_ref, held, mid = rest[:blocks], rest[blocks], rest[blocks + 1], rest[blocks + 2]
    tile = m_ref.shape[0]
    cols = b_ref.shape[2]
    spread_all(l_ref, p_refs, held)

    @pl.loop(0, tile // ROWS)
    def _(i):
        rows = pl.ds(pl.multiple_of(i * ROWS, ROWS), ROWS)
        table, wt = m_ref[rows, :], wt_ref[rows, :]
        terms = [wt[:, v : v + 1] * held[rows, v * cols : (v + 1) * cols] for v in range(nf)]
        got = mix(table, 0, nf, terms)
        for w in range(nf):
            mid[w] = b_ref[w, rows, :] + got[w]
        got = mix(table, 0, nf, [mid[v] for v in range(nf)])
        for w in range(nf):
            u_ref[w, rows, :] = got[w]


def own_kernel(nf, own, blocks, last, l_ref, q_ref, b_ref, *rest):
    if last:
        s_ref, rest = rest[0], rest[1:]
    p_refs, rest = rest[:blocks], rest[blocks:]
    if last:
        a_ref, new_ref, held = rest
    else:
        new_ref, held = rest
    tile = q_ref.shape[0]
    cols = b_ref.shape[2]
    spread_all(l_ref, p_refs, held)

    @pl.loop(0, tile // ROWS)
    def _(i):
        rows = pl.ds(pl.multiple_of(i * ROWS, ROWS), ROWS)
        table = q_ref[rows, :]
        terms = [held[rows, v * cols : (v + 1) * cols] for v in range(nf)]
        got = mix(table, 0, own, terms)
        for w in range(own):
            new_ref[w, rows, :] = b_ref[w, rows, :] + got[w]
            if last:
                col = own * nf + w
                a_ref[w, rows, :] = s_ref[w, rows, :] + table[:, col : col + 1] * terms[w]


def early(table, x):
    nf, pairs, cols = x.shape
    tile = tile_of(pairs)
    spec = pl.BlockSpec((nf, tile, cols), lambda i: (0, i, 0))
    return pl.pallas_call(
        functools.partial(early_kernel, nf),
        out_shape=jax.ShapeDtypeStruct(x.shape, jnp.float32),
        grid=(pairs // tile,),
        in_specs=[pl.BlockSpec((tile, table.shape[1]), lambda i: (i, 0)), spec],
        out_specs=spec,
        cost_estimate=pl.CostEstimate(
            flops=2 * nf * nf * pairs * cols * 8, bytes_accessed=8 * x.size, transcendentals=0
        ),
    )(table, x)


def resident(p):
    return pl.BlockSpec(p.shape, lambda i: (0, 0), pipeline_mode=pl.Buffered(1))


def whole(factors, table, weight, base, projected):
    nf, pairs, cols = base.shape
    tile = tile_of(pairs)
    naux = factors.shape[1]
    spec = pl.BlockSpec((nf, tile, cols), lambda i: (0, i, 0))
    return pl.pallas_call(
        functools.partial(whole_kernel, nf, len(projected)),
        out_shape=jax.ShapeDtypeStruct(base.shape, jnp.float32),
        grid=(pairs // tile,),
        in_specs=[
            pl.BlockSpec((tile, naux), lambda i: (i, 0)),
            pl.BlockSpec((tile, table.shape[1]), lambda i: (i, 0)),
            pl.BlockSpec((tile, weight.shape[1]), lambda i: (i, 0)),
            spec,
        ]
        + [resident(p) for p in projected],
        out_specs=spec,
        scratch_shapes=[
            pltpu.VMEM((tile, nf * cols), jnp.float32),
            pltpu.VMEM((nf, ROWS, cols), jnp.float32),
        ],
        compiler_params=pltpu.CompilerParams(vmem_limit_bytes=56 << 20),
        cost_estimate=pl.CostEstimate(
            flops=2 * nf * pairs * cols * (naux + 16 * nf), bytes_accessed=8 * base.size, transcendentals=0
        ),
    )(factors, table, weight, base, *projected)


def own_part(factors, table, base, projected, nf, sources=None):
    own, pairs, cols = base.shape
    tile = tile_of(pairs)
    naux = factors.shape[1]
    last = sources is not None
    spec = pl.BlockSpec((own, tile, cols), lambda i: (0, i, 0))
    shape = jax.ShapeDtypeStruct(base.shape, jnp.float32)
    return pl.pallas_call(
        functools.partial(own_kernel, nf, own, len(projected), last),
        out_shape=(shape, shape) if last else shape,
        grid=(pairs // tile,),
        in_specs=[
            pl.BlockSpec((tile, naux), lambda i: (i, 0)),
            pl.BlockSpec((tile, table.shape[1]), lambda i: (i, 0)),
            spec,
        ]
        + ([spec] if last else [])
        + [resident(p) for p in projected],
        out_specs=(spec, spec) if last else spec,
        scratch_shapes=[pltpu.VMEM((tile, nf * cols), jnp.float32)],
        compiler_params=pltpu.CompilerParams(vmem_limit_bytes=56 << 20),
        cost_estimate=pl.CostEstimate(
            flops=2 * nf * pairs * cols * naux, bytes_accessed=12 * base.size, transcendentals=0
        ),
    )(factors, table, base, *((sources,) if last else ()), *projected)


def packed(x):
    top = jnp.maximum(jnp.max(jnp.abs(x)), 1e-30)
    return 16384.0 / top, jnp.full((8, 128), top / 16384.0, jnp.float32)


def shards(right_side, factors, pair_weight, second_order, forward, backward):
    own, pairs, cols = right_side.shape
    nf = forward.shape[0]
    parts = nf // own
    quarter = pairs // parts
    me = lax.axis_index("freq")

    def shift(x, by):
        if by == 0:
            return x
        return lax.ppermute(x, "freq", [(i, (i + by) % parts) for i in range(parts)])

    def sliced(x, place, axis):
        return lax.dynamic_slice_in_dim(x, lax.rem(place, parts) * quarter, quarter, axis)

    order = jnp.concatenate(
        [lax.rem(me - s + parts, parts) * own + jnp.arange(own) for s in range(parts)]
    )
    pick = jax.nn.one_hot(order, nf, dtype=jnp.float32)
    ahead = jnp.einsum("ts,sv,wv->tw", pick, forward, pick, precision=EXACT)
    back = jnp.einsum("ws,st,vt->wv", pick, backward, pick, precision=EXACT)
    coefficient = back.T[:, :, None] * ahead[:, None, :]

    up, down = packed(right_side)
    moved = []
    for s in range(parts):
        if s == 0:
            moved.append(sliced(right_side, me, 1))
        else:
            out = (sliced(right_side, me + s, 1) * up).astype(jnp.float16)
            moved.append(shift(out, s).astype(jnp.float32) * shift(down, s)[0, 0])
    both = jnp.stack([pair_weight, second_order])
    tables = jnp.concatenate([shift(both, s) for s in range(parts)], axis=1)
    weights, kernels = tables[0], tables[1]

    def ladder(sources):
        amplitude = sources
        for inner in range(INNER):
            rounded = amplitude.astype(jnp.bfloat16)
            partial_value = jnp.einsum(
                "pa,fpc->fac", factors, rounded, preferred_element_type=jnp.float32
            )
            projected = lax.psum(partial_value, "fac").astype(jnp.bfloat16)
            if inner < INNER - 1:
                spread = jnp.einsum(
                    "pa,fac->fpc", factors, projected, preferred_element_type=jnp.float32
                )
                amplitude = sources + pair_weight[:, :, None] * spread
        mine = jnp.transpose(projected, (1, 0, 2)).reshape(projected.shape[1], own * cols)
        return [shift(mine, s) for s in range(parts)]

    table_own = jnp.einsum(
        "tp,tj->pj", kernels, coefficient[:, :own].reshape(nf, own * nf), precision=EXACT
    )
    weight_rows = weights.T
    table_own = table_own * jnp.tile(weight_rows, (1, own))
    table_own = jnp.concatenate([table_own, weight_rows[:, :own]], axis=1)
    table_all = jnp.einsum(
        "tp,tj->pj", sliced(kernels, me, 1), coefficient.reshape(nf, nf * nf), precision=EXACT
    )
    weight_here = sliced(weight_rows, me, 0)
    factors_here = sliced(factors, me, 0)

    def returned(x):
        scale, unscale = packed(x)
        result = right_side
        for s in range(parts):
            block = x[s * own : (s + 1) * own]
            if s > 0:
                block = shift((block * scale).astype(jnp.float16), parts - s)
                block = block.astype(jnp.float32) * shift(unscale, parts - s)[0, 0]
            at = lax.rem(me + s, parts) * quarter
            result = lax.dynamic_update_slice_in_dim(
                result, lax.dynamic_slice_in_dim(right_side, at, quarter, 1) + block, at, 1
            )
        return result

    right_here = jnp.concatenate(moved, axis=0)
    gain = early(table_all, right_here)
    held_here = right_here + gain

    projected = ladder(right_side)
    base = returned(gain)
    sources = own_part(factors, table_own, base, projected, nf)
    gain = whole(factors_here, table_all, weight_here, held_here, projected)
    projected = ladder(sources)
    base = returned(gain)
    return own_part(factors, table_own, base, projected, nf, sources)


def solution(mesh):
    return jax.shard_map(
        shards,
        mesh=mesh,
        in_specs=(
            P("freq", "fac", None),
            P("fac", None),
            P("freq", "fac"),
            P("freq", "fac"),
            P(),
            P(),
        ),
        out_specs=(P("freq", "fac", None), P("freq", "fac", None)),
        check_vma=False,
    )
```

```python
import functools

import jax
import jax.numpy as jnp
from jax import lax
from jax.experimental import pallas as pl
from jax.experimental.pallas import tpu as pltpu
from jax.sharding import PartitionSpec as P


INNER = 2
LANES = 128
CHUNK = 16
WIDE = 32
EXACT = lax.Precision.HIGHEST


def tile_of(pairs):
    for blocks in (3, 4, 2, 1):
        if pairs % (blocks * LANES) == 0:
            return blocks * LANES
    return None


def mix(table, lanes, outs, count, term):
    totals = [None] * outs
    for v in range(count):
        value = term(v)
        for w in range(outs):
            row = w * count + v
            product = table[row : row + 1, lanes] * value
            totals[w] = product if totals[w] is None else totals[w] + product
    return totals


def blocks_of(ref):
    return [slice(k, k + LANES) for k in range(0, ref.shape[1], LANES)]


def part(i, base, chunk):
    return pl.ds(pl.multiple_of(base + i * chunk, chunk), chunk)


def early_kernel(nf, m_ref, x_ref, v_ref, turned, mid):
    cols = x_ref.shape[2]
    for lanes in blocks_of(m_ref):
        for v in range(nf):
            turned[v] = x_ref[v, lanes, :].T

        @pl.loop(0, cols // CHUNK)
        def _(i):
            rows = part(i, 0, CHUNK)
            got = mix(m_ref, lanes, nf, nf, lambda v: turned[v, rows, :])
            for w in range(nf):
                mid[w, rows, :] = got[w]

        for w in range(nf):
            v_ref[w, lanes, :] = mid[w].T


def spread_all(l_ref, p_refs, held):
    block = p_refs[0].shape[0]
    for i, p_ref in enumerate(p_refs):
        held[i * block : (i + 1) * block, :] = lax.dot_general(
            p_ref[...], l_ref[...], (((1,), (1,)), ((), ())), preferred_element_type=jnp.float32
        )


def whole_kernel(nf, blocks, l_ref, m_ref, wt_ref, b_ref, *rest):
    p_refs, (u_ref, held, turned, mid) = rest[:blocks], rest[blocks:]
    cols = b_ref.shape[2]
    spread_all(l_ref, p_refs, held)
    for lanes in blocks_of(m_ref):
        for v in range(nf):
            turned[v] = b_ref[v, lanes, :].T

        @pl.loop(0, cols // CHUNK)
        def _(i):
            rows = part(i, 0, CHUNK)
            got = mix(
                m_ref,
                lanes,
                nf,
                nf,
                lambda v: wt_ref[v : v + 1, lanes] * held[part(i, v * cols, CHUNK), lanes],
            )
            for w in range(nf):
                turned[w, rows, :] = turned[w, rows, :] + got[w]
            got = mix(m_ref, lanes, nf, nf, lambda v: turned[v, rows, :])
            for w in range(nf):
                mid[w, rows, :] = got[w]

        for w in range(nf):
            u_ref[w, lanes, :] = mid[w].T


def own_kernel(nf, own, blocks, last, l_ref, q_ref, b_ref, *rest):
    if last:
        s_ref, rest = rest[0], rest[1:]
    p_refs, rest = rest[:blocks], rest[blocks:]
    if last:
        a_ref, new_ref, held, mid, second = rest
    else:
        new_ref, held, mid = rest
    cols = b_ref.shape[2]
    spread_all(l_ref, p_refs, held)
    for lanes in blocks_of(q_ref):

        @pl.loop(0, cols // WIDE)
        def _(i):
            rows = part(i, 0, WIDE)
            got = mix(q_ref, lanes, own, nf, lambda v: held[part(i, v * cols, WIDE), lanes])
            for w in range(own):
                mid[w, rows, :] = got[w]
                if last:
                    row = own * nf + w
                    second[w, rows, :] = (
                        q_ref[row : row + 1, lanes] * held[part(i, w * cols, WIDE), lanes]
                    )

        for w in range(own):
            new_ref[w, lanes, :] = b_ref[w, lanes, :] + mid[w].T
            if last:
                a_ref[w, lanes, :] = s_ref[w, lanes, :] + second[w].T


def early(table, x):
    nf, pairs, cols = x.shape
    tile = tile_of(pairs)
    if tile is None:
        return jnp.einsum("wvp,vpc->wpc", table.reshape(nf, nf, pairs), x, precision=EXACT)
    spec = pl.BlockSpec((nf, tile, cols), lambda i: (0, i, 0))
    return pl.pallas_call(
        functools.partial(early_kernel, nf),
        out_shape=jax.ShapeDtypeStruct(x.shape, jnp.float32),
        grid=(pairs // tile,),
        in_specs=[pl.BlockSpec((table.shape[0], tile), lambda i: (0, i)), spec],
        out_specs=spec,
        scratch_shapes=[pltpu.VMEM((nf, cols, LANES), jnp.float32)] * 2,
        cost_estimate=pl.CostEstimate(
            flops=2 * nf * nf * pairs * cols * 8, bytes_accessed=8 * x.size, transcendentals=0
        ),
    )(table, x)


def resident(p):
    return pl.BlockSpec(p.shape, lambda i: (0, 0), pipeline_mode=pl.Buffered(1))


def whole(factors, table, weight, base, projected):
    nf, pairs, cols = base.shape
    tile = tile_of(pairs)
    naux = factors.shape[1]
    if tile is None:
        spread = jnp.einsum(
            "ja,pa->jp", jnp.concatenate(projected), factors, preferred_element_type=jnp.float32
        )
        spread = jnp.transpose(spread.reshape(nf, cols, pairs), (0, 2, 1))
        return early(table, base + early(table, weight[:, :, None] * spread))
    spec = pl.BlockSpec((nf, tile, cols), lambda i: (0, i, 0))
    return pl.pallas_call(
        functools.partial(whole_kernel, nf, len(projected)),
        out_shape=jax.ShapeDtypeStruct(base.shape, jnp.float32),
        grid=(pairs // tile,),
        in_specs=[
            pl.BlockSpec((tile, naux), lambda i: (i, 0)),
            pl.BlockSpec((table.shape[0], tile), lambda i: (0, i)),
            pl.BlockSpec((weight.shape[0], tile), lambda i: (0, i)),
            spec,
        ]
        + [resident(p) for p in projected],
        out_specs=spec,
        scratch_shapes=[
            pltpu.VMEM((nf * cols, tile), jnp.float32),
            pltpu.VMEM((nf, cols, LANES), jnp.float32),
            pltpu.VMEM((nf, cols, LANES), jnp.float32),
        ],
        compiler_params=pltpu.CompilerParams(vmem_limit_bytes=56 << 20),
        cost_estimate=pl.CostEstimate(
            flops=2 * nf * pairs * cols * (naux + 16 * nf), bytes_accessed=8 * base.size, transcendentals=0
        ),
    )(factors, table, weight, base, *projected)


def own_part(factors, table, base, projected, nf, sources=None):
    own, pairs, cols = base.shape
    tile = tile_of(pairs)
    naux = factors.shape[1]
    last = sources is not None
    spec = pl.BlockSpec((own, tile, cols), lambda i: (0, i, 0))
    shape = jax.ShapeDtypeStruct(base.shape, jnp.float32)
    return pl.pallas_call(
        functools.partial(own_kernel, nf, own, len(projected), last),
        out_shape=(shape, shape) if last else shape,
        grid=(pairs // tile,),
        in_specs=[
            pl.BlockSpec((tile, naux), lambda i: (i, 0)),
            pl.BlockSpec((table.shape[0], tile), lambda i: (0, i)),
            spec,
        ]
        + ([spec] if last else [])
        + [resident(p) for p in projected],
        out_specs=(spec, spec) if last else spec,
        scratch_shapes=[pltpu.VMEM((nf * cols, tile), jnp.float32)]
        + [pltpu.VMEM((own, cols, LANES), jnp.float32)] * (2 if last else 1),
        compiler_params=pltpu.CompilerParams(vmem_limit_bytes=56 << 20),
        cost_estimate=pl.CostEstimate(
            flops=2 * nf * pairs * cols * naux, bytes_accessed=12 * base.size, transcendentals=0
        ),
    )(factors, table, base, *((sources,) if last else ()), *projected)


def packed(x):
    top = jnp.maximum(jnp.max(jnp.abs(x)), 1e-30)
    return 16384.0 / top, jnp.full((8, 128), top / 16384.0, jnp.float32)


def shards(right_side, factors, pair_weight, second_order, forward, backward):
    own, pairs, cols = right_side.shape
    nf = forward.shape[0]
    parts = nf // own
    quarter = pairs // parts
    me = lax.axis_index("freq")

    def shift(x, by):
        if by == 0:
            return x
        return lax.ppermute(x, "freq", [(i, (i + by) % parts) for i in range(parts)])

    def sliced(x, place, axis):
        return lax.dynamic_slice_in_dim(x, lax.rem(place, parts) * quarter, quarter, axis)

    order = jnp.concatenate(
        [lax.rem(me - s + parts, parts) * own + jnp.arange(own) for s in range(parts)]
    )
    pick = jax.nn.one_hot(order, nf, dtype=jnp.float32)
    ahead = jnp.einsum("ts,sv,wv->tw", pick, forward, pick, precision=EXACT)
    back = jnp.einsum("ws,st,vt->wv", pick, backward, pick, precision=EXACT)
    coefficient = back.T[:, :, None] * ahead[:, None, :]

    up, down = packed(right_side)
    moved = []
    for s in range(parts):
        if s == 0:
            moved.append(sliced(right_side, me, 1))
        else:
            out = (sliced(right_side, me + s, 1) * up).astype(jnp.float16)
            out = shift(out, s)
            moved.append(out.astype(jnp.float32) * shift(down, s)[0, 0])
    both = jnp.stack([pair_weight, second_order])
    tables = jnp.concatenate([shift(both, s) for s in range(parts)], axis=1)
    weights, kernels = tables[0], tables[1]

    def ladder(sources, beside=()):
        amplitude = sources
        for inner in range(INNER):
            rounded = amplitude.astype(jnp.bfloat16)
            partial_value = jnp.einsum(
                "pa,fpc->fac", factors, rounded, preferred_element_type=jnp.float32
            )
            if inner == INNER - 1 and beside:
                partial_value, beside = lax.optimization_barrier((partial_value, beside))
            projected = lax.psum(partial_value, "fac")
            projected = projected.astype(jnp.bfloat16)
            if inner < INNER - 1:
                spread = jnp.einsum(
                    "pa,fac->fpc", factors, projected, preferred_element_type=jnp.float32
                )
                amplitude = sources + pair_weight[:, :, None] * spread
        mine = jnp.transpose(projected, (0, 2, 1)).reshape(own * cols, projected.shape[1])
        return gathered(mine), beside

    def gathered(mine):
        line = lax.axis_size("fac")
        if line % 2:
            return [shift(mine, s) for s in range(parts)]
        side = lax.rem(lax.axis_index("fac"), 2)
        half = mine.shape[0] // 2
        piece = lax.dynamic_slice_in_dim(mine, side * half, half, 0)
        blocks = [mine]
        for s in range(1, parts):
            got = shift(piece, s)
            other = lax.ppermute(got, "fac", [(i, i ^ 1) for i in range(line)])
            low = jnp.where(side == 0, got, other)
            high = jnp.where(side == 0, other, got)
            blocks.append(jnp.concatenate([low, high]))
        return blocks

    table_own = jnp.einsum(
        "tp,tj->jp", kernels, coefficient[:, :own].reshape(nf, own * nf), precision=EXACT
    )
    table_own = table_own * jnp.tile(weights, (own, 1))
    table_own = jnp.concatenate([table_own, weights[:own]], axis=0)
    table_all = jnp.einsum(
        "tp,tj->jp", sliced(kernels, me, 1), coefficient.reshape(nf, nf * nf), precision=EXACT
    )
    weight_here = sliced(weights, me, 1)
    factors_here = sliced(factors, me, 0)

    def leaving(x):
        scale, unscale = packed(x)
        blocks = [x[s * own : (s + 1) * own] for s in range(parts)]
        return [blocks[0]] + [(b * scale).astype(jnp.float16) for b in blocks[1:]], unscale

    def returned(sent):
        blocks, unscale = sent
        result = right_side
        for s, block in enumerate(blocks):
            if s > 0:
                block = shift(block, parts - s)
                block = block.astype(jnp.float32) * shift(unscale, parts - s)[0, 0]
            at = lax.rem(me + s, parts) * quarter
            result = lax.dynamic_update_slice_in_dim(
                result, lax.dynamic_slice_in_dim(right_side, at, quarter, 1) + block, at, 1
            )
        return result

    right_here = jnp.concatenate(moved, axis=0)
    gain = early(table_all, right_here)
    held_here = right_here + gain

    projected, sent = ladder(right_side, leaving(gain))
    base = returned(sent)
    sources = own_part(factors, table_own, base, projected, nf)
    gain = whole(factors_here, table_all, weight_here, held_here, projected)
    projected, _ = ladder(sources)
    base = returned(leaving(gain))
    return own_part(factors, table_own, base, projected, nf, sources)


def solution(mesh):
    return jax.shard_map(
        shards,
        mesh=mesh,
        in_specs=(
            P("freq", "fac", None),
            P("fac", None),
            P("freq", "fac"),
            P("freq", "fac"),
            P(),
            P(),
        ),
        out_specs=(P("freq", "fac", None), P("freq", "fac", None)),
        check_vma=False,
    )
```
